256 devices in a mesh: req: 32 (over z, y), tp: 8 (over x, core).
Axes of the slice: x: 4, y: 4, z: 8, core: 2. Of those that a mesh axis runs over, the one named last changes fastest.
Arguments:
- attn_heads: bfloat16 [4096, 2048], P('req', 'tp'), may hold values from -6 to 6
- residual_in: bfloat16 [4096, 4096], P('req', 'tp'), may hold values from -45 to 45
- w_out: bfloat16 [2048, 4096], P('tp'), may hold values from -0.125 to 0.125
- gain_attn: float32 [4096], P('tp'), may hold values from 0.1 to 1.9
- router: bfloat16 [4096, 8], P('tp'), may hold values from -0.09375 to 0.09375
- expert_ids: int32 [4096, 2], P('req'), may hold values from 0 to 7, all different within a row; in each aligned block of 64 rows (0 to 63, 64 to 127, ...) at most 24 rows name the same one
- lengths: int32 [32, 5], P('req'), may hold values from 1 to 64, 128 in all within a row
- placement: int32 [16], replicated, may hold values from 0 to 7, as said below
- w_gate_up: bfloat16 [32, 2, 4096, 3584], P('req', None, None, 'tp'), may hold values from -1 to 1, as said below
- w_down: bfloat16 [32, 3584, 4096], P('req', 'tp'), may hold values from -1 to 1, as said below
- gain_final: float32 [4096], P('tp'), may hold values from 0.1 to 1.9
Outputs:
- residual_out: bfloat16 [4096, 4096], P('req', 'tp')
- normed_out: bfloat16 [4096, 4096], P('req', 'tp')
The draws below stay inside these ranges and needn't reach their ends.
Inputs may be any that keep to these rules, and one draw needn't show every extreme that they name: `expert_ids`: in each aligned block of 64 rows no expert is named by more than 24 rows, and the two experts of a row differ. `placement`: every expert is held by exactly two pairs. `w_gate_up`: index 2 s + h holds the h-th half of the hidden units of expert placement[s]; the two pairs of one expert hold equal values. `w_down`: index 2 s + h holds the h-th half of the hidden units of expert placement[s]; the two pairs of one expert hold equal values.
All inputs are finite; a program needn't handle non-finite values.
Results may differ from the reference program's by a relative error of at most 0.014.
Values may be sent and summed in bfloat16 or wider, within the bound.
A program may use at most 128 MiB of HBM per device.

```python
import math
import jax
import jax.numpy as jnp
import numpy as np
from jax import lax

D = 4096
HEADS = 16
HEAD_DIM = 128
FFW = 7168
TOK_DEV = 128
REQ_SLOTS = 5
HALF = 64
EXPERTS = 8
CAP = 24
TOKENS = 4096
N_REQ = 32
N_TP = 8


def pair_experts(key):
    order = jax.random.permutation(jax.random.fold_in(key, 11), N_REQ // 2)
    return (order % EXPERTS).astype(jnp.int32)


def draw_placement(key, part):
    return pair_experts(key)


def device_owner(key):
    return jnp.repeat(pair_experts(key), 2)


def draw_w_gate_up(key, part):
    owner = device_owner(key)
    side = jnp.arange(N_REQ, dtype=jnp.int32) % 2

    def one_device(pair_info):
        expert = pair_info[0]
        half_index = pair_info[1]
        sub_key = jax.random.fold_in(jax.random.fold_in(key, 101 + expert), half_index)
        values = jax.random.truncated_normal(sub_key, -4.0, 4.0, (2, D, FFW // 2), jnp.float32)
        return (values * D ** (-0.5)).astype(jnp.bfloat16)
    return lax.map(one_device, jnp.stack([owner, side], axis=1))


def draw_w_down(key, part):
    owner = device_owner(key)
    side = jnp.arange(N_REQ, dtype=jnp.int32) % 2

    def one_device(pair_info):
        expert = pair_info[0]
        half_index = pair_info[1]
        sub_key = jax.random.fold_in(jax.random.fold_in(key, 301 + expert), half_index)
        values = jax.random.truncated_normal(sub_key, -4.0, 4.0, (FFW // 2, D), jnp.float32)
        return (values * FFW ** (-0.5)).astype(jnp.bfloat16)
    return lax.map(one_device, jnp.stack([owner, side], axis=1))


def draw_residual_in(key, part):
    own_key = jax.random.fold_in(key, 5)
    base_key, row_key, col_key = jax.random.split(own_key, 3)
    column = jnp.arange(D, dtype=jnp.float32) / D
    col_scale = 0.5 * 3.0 ** column * jax.random.uniform(col_key, (D,), jnp.float32, 0.7, 1.4)
    row_scale = 10.0 ** jax.random.uniform(row_key, (TOKENS, 1), jnp.float32, -0.5, 0.5)
    base = jax.random.truncated_normal(base_key, -6.0, 6.0, (TOKENS, D), jnp.float32)
    return (base * row_scale * col_scale).astype(jnp.bfloat16)


def level_of(key, shape, shards, low, largest):
    loudness, own = 1.0, jax.random.fold_in(key, 6)
    for position, shards_of in shards:
        draws = jnp.exp(jax.random.uniform(jax.random.fold_in(own, position), (shards_of,), jnp.float32, low / len(shards), largest / len(shards)))
        loudness = loudness * jnp.repeat(draws, shape[position] // shards_of).reshape([-1 if axis == position else 1 for axis in range(len(shape))])
    return loudness


def split_up(amount, total, reach, slope):
    portions = [(1 << 20) // math.isqrt(rank ** slope) + 1 for rank in range(2, amount + 1)]
    spare, counts = total - reach - (amount - 1), [1] * (amount - 1)
    while spare > 0:
        free = [i for i in range(amount - 1) if counts[i] < reach]
        pool, budget = sum([portions[i] for i in free]), spare
        for i in free:
            extra = min(reach - counts[i], max(1, budget * portions[i] // pool), spare)
            counts[i] = counts[i] + extra
            spare = spare - extra
    return np.array([reach] + counts)


def uneven_parts(key, count, total, limit, lean):
    if count == 2:
        one = jax.random.randint(key, (), max(1, total - limit), min(limit, total - 1) + 1)
        return jnp.stack([one, total - one])
    sizes = jnp.asarray(split_up(count, total, limit, lean), jnp.int32)
    couples = (count - 1) // 2
    giver, sink = sizes[1:1 + 2 * couples:2], sizes[2:2 + 2 * couples:2]
    room = jnp.minimum(giver - 1, limit - sink)
    passed = jax.random.randint(jax.random.fold_in(key, 1), (couples,), 0, 1 << 20) % (room + 1)
    sizes = sizes.at[1:1 + 2 * couples:2].set(giver - passed).at[2:2 + 2 * couples:2].set(sink + passed)
    return sizes[jax.random.permutation(jax.random.fold_in(key, 2), count)]


def deal_out(key, own, number, rows, number_of, top, reach, lean):
    ranking = jax.random.permutation(key, number_of)
    heavy_load, ordinary = portions_of(number_of, rows * top, reach, lean, True), portions_of(number_of, rows * top, reach, lean, False)
    places = jnp.arange(number_of)

    def named(sizes, offset_by):
        used = int((sizes > 0).sum())
        fixed = max(1, used // 4)
        moved = fixed + (places - fixed + offset_by * (used - fixed)) % max(1, number_of - fixed)
        return jnp.zeros((number_of,), jnp.int32).at[ranking[jnp.where(places < fixed, places, moved)]].set(jnp.asarray(sizes, jnp.int32))

    sizes = jnp.where(number % 4 == 0, named(heavy_load, number // 4), named(ordinary, number - number // 4 - 1))
    mixed = jax.random.permutation(jax.random.fold_in(own, 3), number_of)
    giver, taker = mixed[0:number_of // 2 * 2:2], mixed[1:number_of // 2 * 2:2]
    slack = jnp.minimum(sizes[giver] - 1, reach - sizes[taker]) // 2
    slack = jnp.where((giver == ranking[0]) | (taker == ranking[0]) | (sizes[taker] == 0), 0, jnp.maximum(slack, 0))
    moved = jax.random.randint(jax.random.fold_in(own, 4), (number_of // 2,), 0, 1 << 20) % (slack + 1)
    sizes = sizes.at[giver].add(-moved).at[taker].add(moved)
    labels = jnp.searchsorted(jnp.cumsum(sizes), jnp.arange(rows * top), side="right").astype(jnp.int32)
    grid = labels.reshape(top, rows).T
    grid = grid[jax.random.permutation(jax.random.fold_in(own, 1), rows)]
    offset_by = jax.random.randint(jax.random.fold_in(own, 2), (rows, 1), 0, top)
    return jnp.take_along_axis(grid, (jnp.arange(top)[None, :] + offset_by) % top, axis=1)


def portions_of(count, total, limit, skew, full):
    loads = [(1 << 20) // math.isqrt(grade ** skew) + 1 for grade in range(1, count + 1)]
    largest = limit if full else min(limit, max(-(-total // count), total * loads[0] // sum(loads)))
    least = 1 if total - largest >= count - 1 else 0
    counts, spare = [largest] + [least] * (count - 1), total - largest - least * (count - 1)
    while spare > 0:
        movable = [i for i in range(1, count) if counts[i] < largest] or [i for i in range(1, count) if counts[i] < limit]
        pool, left = sum([loads[i] for i in movable]), spare
        for i in movable:
            extra = min(limit - counts[i], max(1, left * loads[i] // pool), spare)
            counts[i] = counts[i] + extra
            spare = spare - extra
    return np.array(counts)


def gaussian(stream_key, extent, spread, reach, cuts=(), kind=jnp.bfloat16):
    result = spread * jax.random.normal(stream_key, extent, jnp.float32)
    if cuts:
        result = result * level_of(stream_key, extent, cuts, -0.22, 0.18)
    return jnp.clip(result, -reach, reach).astype(kind)


def setup_inputs(seed: int = 0) -> dict:
    arg_keys = jax.random.split(jax.random.key(seed), 12)
    attn_heads = gaussian(arg_keys[0], (TOKENS, HEADS * HEAD_DIM), 1.0, 6.0, ((0, 32), (1, 8)))
    residual_in = draw_residual_in(jax.random.fold_in(arg_keys[11], 71), 0)
    w_out = gaussian(arg_keys[2], (HEADS * HEAD_DIM, D), (HEADS * HEAD_DIM) ** -0.5, 0.125, ((0, 8),))
    gain_attn = jnp.clip(1.0 + 0.18 * jax.random.normal(arg_keys[3], (D,), jnp.float32), 0.1, 1.9)
    router = gaussian(arg_keys[4], (D, EXPERTS), D ** -0.5, 0.09375, ((0, 8),))
    expert_ids_keys = jax.random.split(jax.random.fold_in(arg_keys[5], 1), TOKENS // HALF)
    expert_ids_turns = jax.random.permutation(jax.random.fold_in(arg_keys[5], 3), TOKENS // HALF)
    expert_ids = jax.vmap(lambda own, number: deal_out(jax.random.fold_in(arg_keys[5], 2), own, number, HALF, EXPERTS, 2, CAP, 2))(expert_ids_keys, expert_ids_turns).reshape((TOKENS, 2))
    lengths = jax.vmap(lambda own: uneven_parts(own, REQ_SLOTS, TOK_DEV, HALF, 2))(jax.random.split(arg_keys[6], N_REQ)).reshape((N_REQ, REQ_SLOTS)).astype(jnp.int32)
    placement = draw_placement(jax.random.fold_in(arg_keys[11], 71), 0)
    w_gate_up = draw_w_gate_up(jax.random.fold_in(arg_keys[11], 71), 0)
    w_down = draw_w_down(jax.random.fold_in(arg_keys[11], 71), 0)
    gain_final = jnp.clip(1.0 + 0.18 * jax.random.normal(arg_keys[10], (D,), jnp.float32), 0.1, 1.9)
    return {"attn_heads": attn_heads, "residual_in": residual_in, "w_out": w_out, "gain_attn": gain_attn, "router": router, "expert_ids": expert_ids, "lengths": lengths, "placement": placement, "w_gate_up": w_gate_up, "w_down": w_down, "gain_final": gain_final}


epsilon = 1e-05

def inverse_rms(values):
    return lax.rsqrt(lax.optimization_barrier(jnp.mean(values * values, axis=-1, keepdims=True)) + epsilon)

def reference(attn_heads, residual_in, w_out, gain_attn, router, expert_ids, lengths, placement, w_gate_up, w_down, gain_final):
    state = residual_in.astype(jnp.float32) + jnp.dot(attn_heads, w_out, preferred_element_type=jnp.float32)
    normed = state * inverse_rms(state) * gain_attn
    normed_bf = normed.astype(jnp.bfloat16)
    logits = jnp.dot(normed, router.astype(jnp.float32), precision=lax.Precision.HIGHEST)
    chosen = jnp.take_along_axis(logits, expert_ids, axis=1)
    weights = jax.nn.sigmoid(chosen - chosen[:, ::-1])
    row_index = jnp.arange(TOKENS, dtype=jnp.int32)
    positions = row_index % TOK_DEV
    owners = row_index // TOK_DEV
    live_count = TOK_DEV - lengths[:, REQ_SLOTS - 1]
    live_rows = positions < live_count[owners]
    flat_ids = expert_ids.reshape(-1)
    flat_live = jnp.repeat(live_rows, 2)
    most_rows = 2 * N_REQ * CAP
    blocks = 2 * N_TP
    block_units = FFW // blocks

    def one_expert(expert, totals):
        first_pair = jnp.argmax(placement == expert).astype(jnp.int32)
        left_device = 2 * first_pair
        gate_left = lax.dynamic_index_in_dim(w_gate_up, left_device, 0, keepdims=False)
        gate_right = lax.dynamic_index_in_dim(w_gate_up, left_device + 1, 0, keepdims=False)
        gate_full = jnp.concatenate([gate_left, gate_right], axis=2)
        down_left = lax.dynamic_index_in_dim(w_down, left_device, 0, keepdims=False)
        down_right = lax.dynamic_index_in_dim(w_down, left_device + 1, 0, keepdims=False)
        down_full = jnp.concatenate([down_left, down_right], axis=0)
        selected = jnp.logical_and(flat_ids == expert, flat_live)
        picked_rows = jnp.nonzero(selected, size=most_rows, fill_value=0)[0].astype(jnp.int32)
        valid_rows = jnp.arange(most_rows) < jnp.sum(selected.astype(jnp.int32))
        rows_in = normed_bf[picked_rows // 2]
        gate_proj = jnp.dot(rows_in, gate_full[0], preferred_element_type=jnp.float32)
        up_proj = jnp.dot(rows_in, gate_full[1], preferred_element_type=jnp.float32)
        activ = (jax.nn.silu(gate_proj) * up_proj).astype(jnp.bfloat16)
        summed = jnp.zeros((most_rows, D), jnp.float32)
        for block in range(blocks):
            lower = block * block_units
            part_sum = jnp.dot(activ[:, lower:lower + block_units], down_full[lower:lower + block_units], preferred_element_type=jnp.float32)
            rounded = lax.optimization_barrier(part_sum.astype(jnp.bfloat16))
            summed = summed + rounded.astype(jnp.float32)
        summed = summed * valid_rows[:, None].astype(jnp.float32)
        return totals.at[picked_rows].add(summed)
    totals = lax.fori_loop(0, EXPERTS, one_expert, jnp.zeros((2 * TOKENS, D), jnp.float32))
    per_choice = totals.reshape(TOKENS, 2, D)
    mixture = per_choice[:, 0] * weights[:, 0:1] + per_choice[:, 1] * weights[:, 1:2]
    combined = state + mixture
    final_norm = combined * inverse_rms(combined) * gain_final
    return (combined.astype(jnp.bfloat16), final_norm.astype(jnp.bfloat16))
```

```python
import functools

import jax
import jax.numpy as jnp
from jax import lax
from jax.experimental import pallas as pl
from jax.experimental.pallas import tpu as pltpu
from jax.sharding import PartitionSpec as P

MESH = pl.DeviceIdType.MESH
EPS = 1e-05
F32 = jnp.float32
BF16 = jnp.bfloat16
NUM_SEMS = 240
NT = (((1,), (1,)), ((), ()))


def offsets(count):
    order = [0]
    for step in range(1, count // 2 + 1):
        order.append(step)
        if count - step != step:
            order.append(count - step)
    return order[:count]


def mega_kernel(
    dims,
    attn, resid, w_out, gain_a, router_t, ids_t, lengths, placement, w_gu, w_d, gain_f,
    res_out, norm_out,
    wo, wg, wu, wdo, wdp, p_s, p_r, h1_s, h1_r, f1_s, f1_r, stat_s, stat_r, outb, xs,
    act_s, act_r, h_s, h_r, f_s, f_r, qx, ret_s, ret_r, fin_s, fin_r, dt, state_ref, wcol,
    loc, ss, rs,
):
    nreq, ny, nt, rows, feat, hid, cap, groups = dims
    nz, nx = nreq // ny, nt // 2
    full = nt * feat
    half_rows = rows // 2
    pairs = nreq // 2
    ct = cap // 8
    per_group = nreq // groups
    bg = per_group * ct
    grows = bg * 8

    r = lax.axis_index("req")
    t = lax.axis_index("tp")
    z, y = r // ny, r % ny
    x, c = t // 2, t % 2
    xr, xl, xo = (x + 1) % nx, (x + nx - 1) % nx, (x + 2) % nx
    tr, tl, to = xr * 2 + c, xl * 2 + c, xo * 2 + c
    tc = x * 2 + (1 - c)

    counter = [0]
    started = []

    def remote(src, dst, req, tp):
        k = counter[0]
        counter[0] += 1
        copy = pltpu.make_async_remote_copy(
            src_ref=src, dst_ref=dst, send_sem=ss.at[k], recv_sem=rs.at[k],
            device_id=(req, tp), device_id_type=MESH,
        )
        copy.start()
        started.append(copy)
        return copy

    order = [(dz, dy) for dz in offsets(nz) for dy in offsets(ny)]
    dest = [((z + dz) % nz) * ny + (y + dy) % ny for dz, dy in order]
    source = [((z + nz - dz) % nz) * ny + (y + ny - dy) % ny for dz, dy in order]

    barrier = pltpu.get_barrier_semaphore()
    for k in range(1, nt):
        pl.semaphore_signal(barrier, inc=1, device_id=(r, (t + k) % nt), device_id_type=MESH)
    for j in range(1, nreq):
        pl.semaphore_signal(barrier, inc=1, device_id=(dest[j], t), device_id_type=MESH)

    load_wo = pltpu.make_async_copy(w_out, wo, loc.at[0])
    load_wo.start()
    load_wg = pltpu.make_async_copy(w_gu.at[0, 0], wg, loc.at[1])
    load_wu = pltpu.make_async_copy(w_gu.at[0, 1], wu, loc.at[2])
    load_wd = [
        pltpu.make_async_copy(
            w_d.at[0, :, pl.ds(pl.multiple_of((2 * i + c) * feat, feat), feat)], wdo.at[i], loc.at[3 + i]
        )
        for i in range(nx)
    ]

    e_iota = lax.broadcasted_iota(jnp.int32, (8, rows), 0)
    row_iota = lax.broadcasted_iota(jnp.int32, (8, rows), 1)
    live = row_iota < rows - lengths[0, lengths.shape[1] - 1]
    ids = [jnp.broadcast_to(ids_t[k : k + 1, :], (8, rows)) for k in range(2)]
    match = [jnp.where((e_iota == ids[k]) & live, 1.0, 0.0).astype(F32) for k in range(2)]
    hot = match[0] + match[1]
    sub = lax.broadcasted_iota(jnp.int32, (rows, rows), 0)
    lane = lax.broadcasted_iota(jnp.int32, (rows, rows), 1)
    earlier = (sub < lane) & ((sub >= half_rows) == (lane >= half_rows))
    running = jnp.dot(hot.astype(BF16), jnp.where(earlier, 1.0, 0.0).astype(BF16), preferred_element_type=F32)
    seen = jnp.zeros((8, rows), jnp.int32)
    target = jnp.zeros((8, rows), jnp.int32)
    want = jnp.where(row_iota >= half_rows, 1, 0)
    for s in range(pairs):
        held = e_iota == placement[s]
        target = jnp.where(held & (seen == want), s, target)
        seen = seen + jnp.where(held, 1, 0)
    slot = target.astype(F32) * float(cap) + running
    live1 = live[0:1, :]
    keys = [
        jnp.where(live1, jnp.sum(match[k] * slot, axis=0, keepdims=True), -1.0) for k in range(2)
    ]

    def column(vec):
        return jnp.transpose(jnp.broadcast_to(vec, (rows, rows)))

    col = lax.broadcasted_iota(jnp.int32, (8, nreq * cap), 1)
    colkey = jnp.zeros((8, nreq * cap), jnp.int32)
    for j in range(nreq):
        inside = (col >= j * cap) & (col < (j + 1) * cap)
        colkey = jnp.where(inside, (dest[j] // 2) * cap + (col - j * cap), colkey)
    colkey_f = colkey.astype(F32)
    for k in range(2):
        keyc = column(keys[k])
        for b in range(nreq * cap // 128):
            piece = jnp.broadcast_to(colkey_f[0:1, b * 128 : (b + 1) * 128], (rows, 128))
            dt[k, :, b * 128 : (b + 1) * 128] = jnp.where(keyc == piece, 1.0, 0.0).astype(BF16)

    load_wo.wait()
    load_wg.start()
    load_wu.start()
    for copy in load_wd:
        copy.start()
    heads = attn[...]
    for i in range(nx):
        w = wo[:, pl.ds(pl.multiple_of((2 * i + 1 - c) * feat, feat), feat)]
        p_s[i] = jnp.dot(heads, w, preferred_element_type=F32).astype(BF16)

    pl.semaphore_wait(barrier, nt - 1 + nreq - 1)

    p_copy = remote(p_s, p_r, r, tc)

    def own_share(i):
        w = wo[:, pl.ds(pl.multiple_of((2 * i + c) * feat, feat), feat)]
        return jnp.dot(heads, w, preferred_element_type=F32)

    own = [own_share(i) for i in (xo, xr, xl, x)]
    p_copy.wait_recv()
    share = [own[n] + p_r[i].astype(F32) for n, i in enumerate((xo, xr, xl, x))]
    h1_s[0] = share[0][:half_rows].astype(BF16)
    h1_s[1] = share[0][half_rows:].astype(BF16)
    up = remote(h1_s.at[0], h1_r.at[0], r, tr)
    down = remote(h1_s.at[1], h1_r.at[1], r, tl)
    up.wait_recv()
    f1_s[0, :half_rows] = (share[1][:half_rows] + h1_r[0].astype(F32)).astype(BF16)
    f1_s[0, half_rows:] = share[1][half_rows:].astype(BF16)
    fup = remote(f1_s.at[0], f1_r.at[0], r, tr)
    down.wait_recv()
    f1_s[1, :half_rows] = share[2][:half_rows].astype(BF16)
    f1_s[1, half_rows:] = (share[2][half_rows:] + h1_r[1].astype(F32)).astype(BF16)
    fdown = remote(f1_s.at[1], f1_r.at[1], r, tl)
    base = resid[...].astype(F32) + share[3]
    fup.wait_recv()
    fdown.wait_recv()
    state = base + f1_r[0].astype(F32) + f1_r[1].astype(F32)
    state_ref[...] = state

    wd_copies = [
        remote(w_d.at[0, :, pl.ds(pl.multiple_of((2 * i + 1 - c) * feat, feat), feat)], wdp.at[i], r, tc)
        for i in range(nx)
    ]

    ones = jnp.ones((8, feat), F32)
    gain = gain_a[...]

    def square_sums(values):
        return lax.dot_general(ones, values * values, NT, precision=lax.Precision.HIGHEST, preferred_element_type=F32)

    stat_s[0:8] = square_sums(state)
    stat_s[8:16] = lax.dot_general(
        router_t[...] * gain, state, NT, precision=lax.Precision.HIGHEST, preferred_element_type=F32
    )
    stat_copies = [remote(stat_s, stat_r.at[k - 1], r, (t + k) % nt) for k in range(1, nt)]
    total = stat_s[...]
    for k, copy in enumerate(stat_copies):
        copy.wait_recv()
        total = total + stat_r[k]
    inverse = lax.rsqrt(total[0:1] / full + EPS)
    inv_col = jnp.concatenate([column(inverse)] * (feat // rows), axis=1)
    normed = (state * inv_col * gain).astype(BF16)

    slots = lax.broadcasted_iota(jnp.int32, (pairs * cap, rows), 0)
    chosen_slot = (slots == keys[0].astype(jnp.int32)) | (slots == keys[1].astype(jnp.int32))
    scatter = jnp.where(chosen_slot, 1.0, 0.0).astype(BF16)
    sent = jnp.dot(scatter, normed, preferred_element_type=F32)
    outb[...] = sent.reshape(pairs * ct, 8, feat).astype(BF16)

    keep = pltpu.make_async_copy(
        outb.at[pl.ds((r // 2) * ct, ct)], xs.at[t, pl.ds(0, ct)], loc.at[3 + nx]
    )
    keep.start()
    a2a = [None] + [
        remote(outb.at[pl.ds((dest[j] // 2) * ct, ct)], xs.at[t, pl.ds(j * ct, ct)], dest[j], t)
        for j in range(1, nreq)
    ]

    logits = total[8:16] * inverse
    picked = [jnp.sum(match[k] * logits, axis=0, keepdims=True) for k in range(2)]
    wcol[0] = column(jax.nn.sigmoid(picked[0] - picked[1]))
    wcol[1] = column(jax.nn.sigmoid(picked[1] - picked[0]))

    load_wg.wait()
    load_wu.wait()

    gather = {}
    reduce = {}
    returns = {}

    def rows_of(g, part=0, parts=1):
        return pl.ds(g * bg + part * (bg // parts), bg // parts)

    def stage_a(g):
        for j in range(g * per_group, (g + 1) * per_group):
            if j == 0:
                keep.wait()
            else:
                a2a[j].wait_recv()
        mine = xs.at[t, rows_of(g)]
        gather[g, "right"] = remote(mine, mine, r, tr)
        gather[g, "left"] = remote(mine, mine, r, tl)
        gather[g, "own"] = remote(mine, mine, r, tc)

    def stage_b(g):
        gather[g, "right"].wait_recv()
        top = xs.at[tl, rows_of(g, 0, 2)]
        gather[g, "top"] = remote(top, top, r, tr)
        gather[g, "left"].wait_recv()
        bottom = xs.at[tr, rows_of(g, 1, 2)]
        gather[g, "bottom"] = remote(bottom, bottom, r, tl)
        for name, who in (("fwd_l", tl), ("fwd_r", tr)):
            block = xs.at[who, rows_of(g)]
            gather[g, name] = remote(block, block, r, tc)

    def stage_c(g):
        gather[g, "top"].wait_recv()
        gather[g, "bottom"].wait_recv()
        block = xs.at[to, rows_of(g)]
        gather[g, "fwd_o"] = remote(block, block, r, tc)

    def stage_m(g):
        gate = up_acc = None
        plan = (
            (t, None), (tl, None), (tr, None), (to, None),
            (tc, "own"), (xl * 2 + (1 - c), "fwd_l"), (xr * 2 + (1 - c), "fwd_r"), (xo * 2 + (1 - c), "fwd_o"),
        )
        for who, name in plan:
            if name is not None:
                gather[g, name].wait_recv()
            block = xs[who, g * bg : (g + 1) * bg].reshape(grows, feat)
            k_rows = pl.ds(pl.multiple_of(who * feat, feat), feat)
            gp = jnp.dot(block, wg[k_rows, :], preferred_element_type=F32)
            up_p = jnp.dot(block, wu[k_rows, :], preferred_element_type=F32)
            gate = gp if gate is None else gate + gp
            up_acc = up_p if up_acc is None else up_acc + up_p
        act_s[g] = (jax.nn.silu(gate) * up_acc).astype(BF16)
        reduce[g, "act"] = remote(act_s.at[g], act_r.at[g], r, tc)

    def product(g, i):
        own_part = jnp.dot(act_s[g], wdo[i], preferred_element_type=F32)
        return own_part + jnp.dot(act_r[g], wdp[i], preferred_element_type=F32)

    gh = grows // 2

    def stage_d(g):
        reduce[g, "act"].wait_recv()
        far = product(g, xo).astype(BF16)
        h_s[g, 0] = far[:gh]
        h_s[g, 1] = far[gh:]
        reduce[g, "up"] = remote(h_s.at[g, 0], h_r.at[g, 0], r, tr)
        reduce[g, "down"] = remote(h_s.at[g, 1], h_r.at[g, 1], r, tl)

    def stage_e(g):
        near = product(g, xr)
        reduce[g, "up"].wait_recv()
        f_s[g, 0, :gh] = (near[:gh] + h_r[g, 0].astype(F32)).astype(BF16)
        f_s[g, 0, gh:] = near[gh:].astype(BF16)
        reduce[g, "fup"] = remote(f_s.at[g, 0], f_r.at[g, 0], r, tr)
        near = product(g, xl)
        reduce[g, "down"].wait_recv()
        f_s[g, 1, :gh] = near[:gh].astype(BF16)
        f_s[g, 1, gh:] = (near[gh:] + h_r[g, 1].astype(F32)).astype(BF16)
        reduce[g, "fdown"] = remote(f_s.at[g, 1], f_r.at[g, 1], r, tl)
        qx[g] = product(g, x)

    def stage_f(g):
        reduce[g, "fup"].wait_recv()
        reduce[g, "fdown"].wait_recv()
        result = qx[g] + f_r[g, 0].astype(F32) + f_r[g, 1].astype(F32)
        ret_s[g * bg : (g + 1) * bg] = result.reshape(bg, 8, feat).astype(BF16)
        for j in range(g * per_group, (g + 1) * per_group):
            if j == 0:
                returns[0] = pltpu.make_async_copy(ret_s.at[pl.ds(0, ct)], ret_r.at[pl.ds(0, ct)], loc.at[4 + nx])
                returns[0].start()
            else:
                block = pl.ds(j * ct, ct)
                returns[j] = remote(ret_s.at[block], ret_r.at[block], source[j], t)

    def load_down():
        for copy in load_wd:
            copy.wait()
        for copy in wd_copies:
            copy.wait_recv()

    stage_a(0)
    stage_a(1)
    stage_b(0)
    stage_c(0)
    stage_b(1)
    stage_m(0)
    stage_a(2)
    load_down()
    stage_d(0)
    stage_c(1)
    stage_m(1)
    stage_e(0)
    stage_b(2)
    stage_a(3)
    stage_d(1)
    stage_c(2)
    stage_f(0)
    stage_m(2)
    stage_b(3)
    stage_e(1)
    stage_d(2)
    stage_c(3)
    stage_f(1)
    stage_m(3)
    stage_e(2)
    stage_d(3)
    stage_e(3)
    stage_f(2)
    stage_f(3)

    mix = [None, None]
    half = nreq // 2
    for part in range(2):
        for j in range(part * half, (part + 1) * half):
            if j == 0:
                returns[0].wait()
            else:
                returns[j].wait_recv()
        block = ret_r[part * half * ct : (part + 1) * half * ct].reshape(half * cap, feat)
        for k in range(2):
            pick = dt[k, :, part * half * cap : (part + 1) * half * cap]
            got = jnp.dot(pick, block, preferred_element_type=F32)
            mix[k] = got if mix[k] is None else mix[k] + got
    wide = [jnp.concatenate([wcol[k]] * (feat // rows), axis=1) for k in range(2)]
    combined = state_ref[...] + mix[0] * wide[0] + mix[1] * wide[1]
    res_out[...] = combined.astype(BF16)
    fin_s[...] = square_sums(combined)
    fin_copies = [remote(fin_s, fin_r.at[k - 1], r, (t + k) % nt) for k in range(1, nt)]
    total = fin_s[...]
    for k, copy in enumerate(fin_copies):
        copy.wait_recv()
        total = total + fin_r[k]
    scale = lax.rsqrt(total[0:1] / full + EPS)
    scale_col = jnp.concatenate([column(scale)] * (feat // rows), axis=1)
    norm_out[...] = (combined * scale_col * gain_f[...]).astype(BF16)
    for copy in started:
        copy.wait_send()
    assert counter[0] <= NUM_SEMS, counter[0]


def on_device(
    attn_heads, residual_in, w_out, gain_attn, router, expert_ids, lengths, placement, w_gate_up, w_down, gain_final
):
    rows = attn_heads.shape[0]
    feat = residual_in.shape[1]
    heads = attn_heads.shape[1]
    nt = lax.axis_size("tp")
    nreq = lax.axis_size("req")
    full = feat * nt
    hid = w_gate_up.shape[3]
    experts = nreq // 4
    cap = min(rows // 2, 3 * rows // (2 * experts))
    groups = 4
    ny = 4
    nx = nt // 2
    ct = cap // 8
    pairs = nreq // 2
    grows = nreq * cap // groups
    router_t = router.astype(F32).T
    if experts < 8:
        router_t = jnp.pad(router_t, ((0, 8 - experts), (0, 0)))
    vmem = pl.BlockSpec(memory_space=pltpu.VMEM)
    smem = pl.BlockSpec(memory_space=pltpu.SMEM)
    hbm = pl.BlockSpec(memory_space=pl.ANY)
    dims = (nreq, ny, nt, rows, feat, hid, cap, groups)
    out = jax.ShapeDtypeStruct((rows, feat), BF16)
    return pl.pallas_call(
        functools.partial(mega_kernel, dims),
        out_shape=(out, out),
        in_specs=[vmem, vmem, hbm, vmem, vmem, vmem, smem, smem, hbm, hbm, vmem],
        out_specs=(vmem, vmem),
        scratch_shapes=[
            pltpu.VMEM((heads, full), BF16),
            pltpu.VMEM((full, hid), BF16),
            pltpu.VMEM((full, hid), BF16),
            pltpu.VMEM((nx, hid, feat), BF16),
            pltpu.VMEM((nx, hid, feat), BF16),
            pltpu.VMEM((nx, rows, feat), BF16),
            pltpu.VMEM((nx, rows, feat), BF16),
            pltpu.VMEM((2, rows // 2, feat), BF16),
            pltpu.VMEM((2, rows // 2, feat), BF16),
            pltpu.VMEM((2, rows, feat), BF16),
            pltpu.VMEM((2, rows, feat), BF16),
            pltpu.VMEM((16, rows), F32),
            pltpu.VMEM((nt - 1, 16, rows), F32),
            pltpu.VMEM((pairs * ct, 8, feat), BF16),
            pltpu.VMEM((nt, nreq * ct, 8, feat), BF16),
            pltpu.VMEM((groups, grows, hid), BF16),
            pltpu.VMEM((groups, grows, hid), BF16),
            pltpu.VMEM((groups, 2, grows // 2, feat), BF16),
            pltpu.VMEM((groups, 2, grows // 2, feat), BF16),
            pltpu.VMEM((groups, 2, grows, feat), BF16),
            pltpu.VMEM((groups, 2, grows, feat), BF16),
            pltpu.VMEM((groups, grows, feat), F32),
            pltpu.VMEM((nreq * ct, 8, feat), BF16),
            pltpu.VMEM((nreq * ct, 8, feat), BF16),
            pltpu.VMEM((8, rows), F32),
            pltpu.VMEM((nt - 1, 8, rows), F32),
            pltpu.VMEM((2, rows, nreq * cap), BF16),
            pltpu.VMEM((rows, feat), F32),
            pltpu.VMEM((2, rows, rows), F32),
            pltpu.SemaphoreType.DMA((5 + nx,)),
            pltpu.SemaphoreType.DMA((NUM_SEMS,)),
            pltpu.SemaphoreType.DMA((NUM_SEMS,)),
        ],
        compiler_params=pltpu.CompilerParams(
            collective_id=0, has_side_effects=True, vmem_limit_bytes=60 * 1024 * 1024
        ),
    )(
        attn_heads,
        residual_in,
        w_out,
        gain_attn.reshape(1, feat),
        router_t,
        expert_ids.T,
        lengths,
        placement,
        w_gate_up,
        w_down,
        gain_final.reshape(1, feat),
    )


def solution(mesh):
    placed = (
        P("req", "tp"),
        P("req", "tp"),
        P("tp", None),
        P("tp"),
        P("tp", None),
        P("req", None),
        P("req", None),
        P(),
        P("req", None, None, "tp"),
        P("req", "tp", None),
        P("tp"),
    )
    return jax.shard_map(
        on_device,
        mesh=mesh,
        in_specs=placed,
        out_specs=(P("req", "tp"), P("req", "tp")),
        check_vma=False,
    )
```

```python
import functools

import jax
import jax.numpy as jnp
from jax import lax
from jax.experimental import pallas as pl
from jax.experimental.pallas import tpu as pltpu
from jax.sharding import PartitionSpec as P

MESH = pl.DeviceIdType.MESH
EPS = 1e-05
F32 = jnp.float32
BF16 = jnp.bfloat16
NUM_SEMS = 240
NT = (((1,), (1,)), ((), ()))


def offsets(count):
    order = [0]
    for step in range(1, count // 2 + 1):
        order.append(step)
        if count - step != step:
            order.append(count - step)
    return order[:count]


def mega_kernel(
    dims,
    attn, resid, w_out, gain_a, router_t, ids_t, lengths, placement, w_gu, w_d,
    res_out, scale_out,
    wo, wg, wu, wdo, wdp, p_s, p_r, h1_s, h1_r, f1_s, f1_r, stat_s, stat_r, outb, xs,
    act_s, act_r, h_s, h_r, f_s, f_r, qx, y_s, y_r, ret_s, ret_r, fin_s, fin_r, dt, state_ref, wcol,
    loc, ss, rs,
):
    nreq, ny, nt, rows, feat, hid, cap, groups = dims
    nz, nx = nreq // ny, nt // 2
    full = nt * feat
    half_rows = rows // 2
    pairs = nreq // 2
    ct = cap // 8
    direct = nreq // 2
    per_group = direct // groups
    bh = per_group * ct
    bg = 2 * bh
    grows = bg * 8
    gh = grows // 2

    r = lax.axis_index("req")
    t = lax.axis_index("tp")
    z, y = r // ny, r % ny
    x, c = t // 2, t % 2
    xr, xl, xo = (x + 1) % nx, (x + nx - 1) % nx, (x + 2) % nx
    tr, tl, to = xr * 2 + c, xl * 2 + c, xo * 2 + c
    tc = x * 2 + (1 - c)
    sibling = (r // 2) * 2 + (1 - r % 2)

    counter = [0]
    started = []

    def remote(src, dst, req, tp):
        k = counter[0]
        counter[0] += 1
        copy = pltpu.make_async_remote_copy(
            src_ref=src, dst_ref=dst, send_sem=ss.at[k], recv_sem=rs.at[k],
            device_id=(req, tp), device_id_type=MESH,
        )
        copy.start()
        started.append(copy)
        return copy

    order = [(dz, q) for dz in offsets(nz) for q in range(2)]
    row_y = (y, ny - 1 - y)
    dest = [((z + dz) % nz) * ny + row_y[q] for dz, q in order]
    source = [((z + nz - dz) % nz) * ny + row_y[q] for dz, q in order]

    barrier = pltpu.get_barrier_semaphore()
    for k in range(1, nt):
        pl.semaphore_signal(barrier, inc=1, device_id=(r, (t + k) % nt), device_id_type=MESH)
    for j in range(1, direct):
        pl.semaphore_signal(barrier, inc=1, device_id=(dest[j], t), device_id_type=MESH)
    pl.semaphore_signal(barrier, inc=1, device_id=(sibling, t), device_id_type=MESH)

    load_wo = pltpu.make_async_copy(w_out, wo, loc.at[0])
    load_wo.start()
    load_wg = pltpu.make_async_copy(w_gu.at[0, 0], wg, loc.at[1])
    load_wu = pltpu.make_async_copy(w_gu.at[0, 1], wu, loc.at[2])
    load_wd = [
        pltpu.make_async_copy(
            w_d.at[0, :, pl.ds(pl.multiple_of((2 * i + c) * feat, feat), feat)], wdo.at[i], loc.at[3 + i]
        )
        for i in range(nx)
    ]

    load_wo.wait()
    load_wg.start()
    load_wu.start()
    for copy in load_wd:
        copy.start()
    heads = attn[...]
    for i in range(nx):
        w = wo[:, pl.ds(pl.multiple_of((2 * i + 1 - c) * feat, feat), feat)]
        p_s[i] = jnp.dot(heads, w, preferred_element_type=F32).astype(BF16)

    pl.semaphore_wait(barrier, nt - 1 + direct)

    p_copy = remote(p_s, p_r, r, tc)

    def own_share(i):
        w = wo[:, pl.ds(pl.multiple_of((2 * i + c) * feat, feat), feat)]
        return jnp.dot(heads, w, preferred_element_type=F32)

    own = [own_share(i) for i in (xo, xr, xl, x)]
    p_copy.wait_recv()
    share = [own[n] + p_r[i].astype(F32) for n, i in enumerate((xo, xr, xl, x))]
    h1_s[0] = share[0][:half_rows].astype(BF16)
    h1_s[1] = share[0][half_rows:].astype(BF16)
    up = remote(h1_s.at[0], h1_r.at[0], r, tr)
    down = remote(h1_s.at[1], h1_r.at[1], r, tl)
    low, high = pl.ds(0, half_rows), pl.ds(half_rows, half_rows)
    f1_s[0, half_rows:] = share[1][half_rows:].astype(BF16)
    f1_s[1, :half_rows] = share[2][:half_rows].astype(BF16)
    first = [
        remote(f1_s.at[0, high], f1_r.at[0, high], r, tr),
        remote(f1_s.at[1, low], f1_r.at[1, low], r, tl),
    ]
    up.wait_recv()
    f1_s[0, :half_rows] = (share[1][:half_rows] + h1_r[0].astype(F32)).astype(BF16)
    first.append(remote(f1_s.at[0, low], f1_r.at[0, low], r, tr))
    down.wait_recv()
    f1_s[1, half_rows:] = (share[2][half_rows:] + h1_r[1].astype(F32)).astype(BF16)
    first.append(remote(f1_s.at[1, high], f1_r.at[1, high], r, tl))

    e_iota = lax.broadcasted_iota(jnp.int32, (8, rows), 0)
    row_iota = lax.broadcasted_iota(jnp.int32, (8, rows), 1)
    live = row_iota < rows - lengths[0, lengths.shape[1] - 1]
    ids = [jnp.broadcast_to(ids_t[k : k + 1, :], (8, rows)) for k in range(2)]
    match = [jnp.where((e_iota == ids[k]) & live, 1.0, 0.0).astype(F32) for k in range(2)]
    hot = match[0] + match[1]
    sub = lax.broadcasted_iota(jnp.int32, (rows, rows), 0)
    lane = lax.broadcasted_iota(jnp.int32, (rows, rows), 1)
    earlier = (sub < lane) & ((sub >= half_rows) == (lane >= half_rows))
    running = jnp.dot(hot.astype(BF16), jnp.where(earlier, 1.0, 0.0).astype(BF16), preferred_element_type=F32)
    seen = jnp.zeros((8, rows), jnp.int32)
    target = jnp.zeros((8, rows), jnp.int32)
    want = jnp.where(row_iota >= half_rows, 1, 0)
    for s in range(pairs):
        held = e_iota == placement[s]
        target = jnp.where(held & (seen == want), s, target)
        seen = seen + jnp.where(held, 1, 0)
    slot = target.astype(F32) * float(cap) + running
    live1 = live[0:1, :]
    keys = [
        jnp.where(live1, jnp.sum(match[k] * slot, axis=0, keepdims=True), -1.0) for k in range(2)
    ]

    def column(vec):
        return jnp.transpose(jnp.broadcast_to(vec, (rows, rows)))

    col = lax.broadcasted_iota(jnp.int32, (8, direct * cap), 1)
    colkey = jnp.zeros((8, direct * cap), jnp.int32)
    for j in range(direct):
        inside = (col >= j * cap) & (col < (j + 1) * cap)
        colkey = jnp.where(inside, (dest[j] // 2) * cap + (col - j * cap), colkey)
    colkey_f = colkey.astype(F32)
    for k in range(2):
        keyc = column(keys[k])
        for b in range(direct * cap // 128):
            piece = jnp.broadcast_to(colkey_f[0:1, b * 128 : (b + 1) * 128], (rows, 128))
            dt[k, :, b * 128 : (b + 1) * 128] = jnp.where(keyc == piece, 1.0, 0.0).astype(BF16)

    base = resid[...].astype(F32) + share[3]
    for copy in first:
        copy.wait_recv()
    state = base + f1_r[0].astype(F32) + f1_r[1].astype(F32)
    state_ref[...] = state

    wd_copies = [
        remote(w_d.at[0, :, pl.ds(pl.multiple_of((2 * i + 1 - c) * feat, feat), feat)], wdp.at[i], r, tc)
        for i in range(nx)
    ]

    ones = jnp.ones((8, feat), F32)
    gain = gain_a[...]

    def square_sums(values):
        return lax.dot_general(ones, values * values, NT, precision=lax.Precision.HIGHEST, preferred_element_type=F32)

    stat_s[0:8] = square_sums(state)
    stat_s[8:16] = lax.dot_general(
        router_t[...].astype(F32) * gain, state, NT, precision=lax.Precision.HIGHEST, preferred_element_type=F32
    )
    stat_copies = [remote(stat_s, stat_r.at[k - 1], r, (t + k) % nt) for k in range(1, nt)]
    total = stat_s[...]
    for k, copy in enumerate(stat_copies):
        copy.wait_recv()
        total = total + stat_r[k]
    inverse = lax.rsqrt(total[0:1] / full + EPS)
    inv_col = jnp.concatenate([column(inverse)] * (feat // rows), axis=1)
    normed = (state * inv_col * gain).astype(BF16)

    slots = lax.broadcasted_iota(jnp.int32, (pairs * cap, rows), 0)
    chosen_slot = (slots == keys[0].astype(jnp.int32)) | (slots == keys[1].astype(jnp.int32))
    scatter = jnp.where(chosen_slot, 1.0, 0.0).astype(BF16)
    sent = jnp.dot(scatter, normed, preferred_element_type=F32)
    outb[...] = sent.reshape(pairs * ct, 8, feat).astype(BF16)

    keep = pltpu.make_async_copy(
        outb.at[pl.ds((r // 2) * ct, ct)], xs.at[t, pl.ds(0, ct)], loc.at[3 + nx]
    )
    keep.start()
    def spot(j):
        return pl.ds((j // per_group) * bg + (j % per_group) * ct, ct)

    a2a = [None] + [
        remote(outb.at[pl.ds((dest[j] // 2) * ct, ct)], xs.at[t, spot(j)], dest[j], t) for j in range(1, direct)
    ]

    logits = total[8:16] * inverse
    picked = [jnp.sum(match[k] * logits, axis=0, keepdims=True) for k in range(2)]
    wcol[0] = column(jax.nn.sigmoid(picked[0] - picked[1]))
    wcol[1] = column(jax.nn.sigmoid(picked[1] - picked[0]))

    load_wg.wait()
    load_wu.wait()

    gather = {}
    reduce = {}
    returns = {}

    def rows_of(g):
        return pl.ds(g * bg, bg)

    def top_of(g):
        return pl.ds(g * bg, bh)

    def low_of(g):
        return pl.ds(g * bg + bh, bh)

    def stage_a(g):
        for j in range(g * per_group, (g + 1) * per_group):
            if j == 0:
                keep.wait()
            else:
                a2a[j].wait_recv()
        mine = xs.at[t, top_of(g)]
        gather[g, "pair"] = remote(mine, xs.at[t, low_of(g)], sibling, t)
        gather[g, "top_r"] = remote(mine, mine, r, tr)
        gather[g, "top_l"] = remote(mine, mine, r, tl)

    def stage_y(g):
        gather[g, "pair"].wait_recv()
        mine = xs.at[t, low_of(g)]
        gather[g, "low_l"] = remote(mine, mine, r, tl)
        gather[g, "low_r"] = remote(mine, mine, r, tr)
        mine = xs.at[t, rows_of(g)]
        gather[g, "own"] = remote(mine, mine, r, tc)

    def stage_b(g):
        gather[g, "top_r"].wait_recv()
        block = xs.at[tl, top_of(g)]
        gather[g, "top"] = remote(block, block, r, tr)
        gather[g, "low_l"].wait_recv()
        block = xs.at[tr, low_of(g)]
        gather[g, "low"] = remote(block, block, r, tl)
        gather[g, "top_l"].wait_recv()
        gather[g, "low_r"].wait_recv()
        for name, who in (("fwd_l", tl), ("fwd_r", tr)):
            block = xs.at[who, rows_of(g)]
            gather[g, name] = remote(block, block, r, tc)

    def stage_c(g):
        gather[g, "top"].wait_recv()
        gather[g, "low"].wait_recv()
        block = xs.at[to, rows_of(g)]
        gather[g, "fwd_o"] = remote(block, block, r, tc)

    def stage_m(g):
        gate = up_acc = None
        plan = (
            (t, None), (tl, None), (tr, None), (to, None),
            (tc, "own"), (xl * 2 + (1 - c), "fwd_l"), (xr * 2 + (1 - c), "fwd_r"), (xo * 2 + (1 - c), "fwd_o"),
        )
        for who, name in plan:
            if name is not None:
                gather[g, name].wait_recv()
            block = xs[who, g * bg : (g + 1) * bg].reshape(grows, feat)
            k_cols = pl.ds(pl.multiple_of(who * feat, feat), feat)
            gp = lax.dot_general(block, wg[:, k_cols], NT, preferred_element_type=F32)
            up_p = lax.dot_general(block, wu[:, k_cols], NT, preferred_element_type=F32)
            gate = gp if gate is None else gate + gp
            up_acc = up_p if up_acc is None else up_acc + up_p
        act_s[g] = (jax.nn.silu(gate) * up_acc).astype(BF16)
        reduce[g, "act"] = remote(act_s.at[g], act_r.at[g], r, tc)

    def product(g, i):
        own_part = jnp.dot(act_s[g], wdo[i], preferred_element_type=F32)
        return own_part + jnp.dot(act_r[g], wdp[i], preferred_element_type=F32)

    def stage_d(g):
        reduce[g, "act"].wait_recv()
        far = product(g, xo).astype(BF16)
        h_s[g, 0] = far[:gh]
        h_s[g, 1] = far[gh:]
        reduce[g, "up"] = remote(h_s.at[g, 0], h_r.at[g, 0], r, tr)
        reduce[g, "down"] = remote(h_s.at[g, 1], h_r.at[g, 1], r, tl)

    def stage_e(g):
        near_r = product(g, xr)
        f_s[g, 0, gh:] = near_r[gh:].astype(BF16)
        reduce[g, "r_high"] = remote(f_s.at[g, 0, pl.ds(gh, gh)], f_r.at[g, 0, pl.ds(gh, gh)], r, tr)
        near_l = product(g, xl)
        f_s[g, 1, :gh] = near_l[:gh].astype(BF16)
        reduce[g, "l_low"] = remote(f_s.at[g, 1, pl.ds(0, gh)], f_r.at[g, 1, pl.ds(0, gh)], r, tl)
        reduce[g, "up"].wait_recv()
        f_s[g, 0, :gh] = (near_r[:gh] + h_r[g, 0].astype(F32)).astype(BF16)
        reduce[g, "r_low"] = remote(f_s.at[g, 0, pl.ds(0, gh)], f_r.at[g, 0, pl.ds(0, gh)], r, tr)
        reduce[g, "down"].wait_recv()
        f_s[g, 1, gh:] = (near_l[gh:] + h_r[g, 1].astype(F32)).astype(BF16)
        reduce[g, "l_high"] = remote(f_s.at[g, 1, pl.ds(gh, gh)], f_r.at[g, 1, pl.ds(gh, gh)], r, tl)
        qx[g] = product(g, x)

    def stage_f(g):
        for name in ("r_high", "l_low", "r_low", "l_high"):
            reduce[g, name].wait_recv()
        low = qx[g, gh:] + f_r[g, 0, gh:].astype(F32) + f_r[g, 1, gh:].astype(F32)
        y_s[g] = low.astype(BF16)
        reduce[g, "pair"] = remote(y_s.at[g], y_r.at[g], sibling, t)
        qx[g, :gh] = qx[g, :gh] + f_r[g, 0, :gh].astype(F32) + f_r[g, 1, :gh].astype(F32)

    def stage_h(g):
        reduce[g, "pair"].wait_recv()
        result = qx[g, :gh] + y_r[g].astype(F32)
        ret_s[g * bh : (g + 1) * bh] = result.reshape(bh, 8, feat).astype(BF16)
        for j in range(g * per_group, (g + 1) * per_group):
            block = pl.ds(j * ct, ct)
            if j == 0:
                returns[0] = pltpu.make_async_copy(ret_s.at[block], ret_r.at[block], loc.at[4 + nx])
                returns[0].start()
            else:
                returns[j] = remote(ret_s.at[block], ret_r.at[block], source[j], t)

    def load_down():
        for copy in load_wd:
            copy.wait()
        for copy in wd_copies:
            copy.wait_recv()

    stage_a(0)
    stage_a(1)
    stage_y(0)
    stage_y(1)
    stage_b(0)
    stage_a(2)
    stage_y(2)
    stage_c(0)
    stage_b(1)
    stage_m(0)
    load_down()
    stage_d(0)
    stage_a(3)
    stage_y(3)
    stage_c(1)
    stage_b(2)
    stage_m(1)
    stage_e(0)
    stage_d(1)
    stage_c(2)
    stage_f(0)
    stage_b(3)
    stage_m(2)
    stage_e(1)
    stage_d(2)
    stage_h(0)
    stage_c(3)
    stage_f(1)
    stage_m(3)
    stage_e(2)
    stage_d(3)
    stage_h(1)
    stage_e(3)
    stage_f(2)
    stage_f(3)
    stage_h(2)
    stage_h(3)

    mix = [None, None]
    half = direct // 2
    for part in range(2):
        for j in range(part * half, (part + 1) * half):
            if j == 0:
                returns[0].wait()
            else:
                returns[j].wait_recv()
        block = ret_r[part * half * ct : (part + 1) * half * ct].reshape(half * cap, feat)
        for k in range(2):
            pick = dt[k, :, part * half * cap : (part + 1) * half * cap]
            got = jnp.dot(pick, block, preferred_element_type=F32)
            mix[k] = got if mix[k] is None else mix[k] + got
    wide = [jnp.concatenate([wcol[k]] * (feat // rows), axis=1) for k in range(2)]
    combined = state_ref[...] + mix[0] * wide[0] + mix[1] * wide[1]
    res_out[...] = combined
    fin_s[...] = square_sums(combined)
    fin_copies = [remote(fin_s, fin_r.at[k - 1], r, (t + k) % nt) for k in range(1, nt)]
    total = fin_s[...]
    for k, copy in enumerate(fin_copies):
        copy.wait_recv()
        total = total + fin_r[k]
    scale = lax.rsqrt(total[0:1] / full + EPS)
    scale_out[...] = jnp.concatenate([column(scale)] * (feat // rows), axis=1)
    for copy in started:
        copy.wait_send()
    assert counter[0] <= NUM_SEMS, counter[0]


def on_device(
    attn_heads, residual_in, w_out, gain_attn, router, expert_ids, lengths, placement, w_gate_up, w_down, gain_final
):
    rows = attn_heads.shape[0]
    feat = residual_in.shape[1]
    heads = attn_heads.shape[1]
    nt = lax.axis_size("tp")
    nreq = lax.axis_size("req")
    full = feat * nt
    hid = w_gate_up.shape[3]
    experts = nreq // 4
    cap = min(rows // 2, 3 * rows // (2 * experts))
    groups = 4
    ny = 4
    nx = nt // 2
    ct = cap // 8
    pairs = nreq // 2
    grows = nreq * cap // groups
    router_t = router.T
    if experts < 8:
        router_t = jnp.pad(router_t, ((0, 8 - experts), (0, 0)))
    vmem = pl.BlockSpec(memory_space=pltpu.VMEM)
    smem = pl.BlockSpec(memory_space=pltpu.SMEM)
    hbm = pl.BlockSpec(memory_space=pl.ANY)
    dims = (nreq, ny, nt, rows, feat, hid, cap, groups)
    combined, scale = pl.pallas_call(
        functools.partial(mega_kernel, dims),
        out_shape=(
            jax.ShapeDtypeStruct((rows, feat), F32),
            jax.ShapeDtypeStruct((rows, feat), F32),
        ),
        in_specs=[vmem, vmem, hbm, vmem, vmem, vmem, smem, smem, hbm, hbm],
        out_specs=(vmem, vmem),
        scratch_shapes=[
            pltpu.VMEM((heads, full), BF16),
            pltpu.VMEM((hid, full), BF16),
            pltpu.VMEM((hid, full), BF16),
            pltpu.VMEM((nx, hid, feat), BF16),
            pltpu.VMEM((nx, hid, feat), BF16),
            pltpu.VMEM((nx, rows, feat), BF16),
            pltpu.VMEM((nx, rows, feat), BF16),
            pltpu.VMEM((2, rows // 2, feat), BF16),
            pltpu.VMEM((2, rows // 2, feat), BF16),
            pltpu.VMEM((2, rows, feat), BF16),
            pltpu.VMEM((2, rows, feat), BF16),
            pltpu.VMEM((16, rows), F32),
            pltpu.VMEM((nt - 1, 16, rows), F32),
            pltpu.VMEM((pairs * ct, 8, feat), BF16),
            pltpu.VMEM((nt, nreq * ct, 8, feat), BF16),
            pltpu.VMEM((groups, grows, hid), BF16),
            pltpu.VMEM((groups, grows, hid), BF16),
            pltpu.VMEM((groups, 2, grows // 2, feat), BF16),
            pltpu.VMEM((groups, 2, grows // 2, feat), BF16),
            pltpu.VMEM((groups, 2, grows, feat), BF16),
            pltpu.VMEM((groups, 2, grows, feat), BF16),
            pltpu.VMEM((groups, grows, feat), F32),
            pltpu.VMEM((groups, grows // 2, feat), BF16),
            pltpu.VMEM((groups, grows // 2, feat), BF16),
            pltpu.VMEM((pairs * ct, 8, feat), BF16),
            pltpu.VMEM((pairs * ct, 8, feat), BF16),
            pltpu.VMEM((8, rows), F32),
            pltpu.VMEM((nt - 1, 8, rows), F32),
            pltpu.VMEM((2, rows, pairs * cap), BF16),
            pltpu.VMEM((rows, feat), F32),
            pltpu.VMEM((2, rows, rows), F32),
            pltpu.SemaphoreType.DMA((5 + nx,)),
            pltpu.SemaphoreType.DMA((NUM_SEMS,)),
            pltpu.SemaphoreType.DMA((NUM_SEMS,)),
        ],
        compiler_params=pltpu.CompilerParams(
            collective_id=0, has_side_effects=True, vmem_limit_bytes=60 * 1024 * 1024
        ),
    )(
        attn_heads,
        residual_in,
        w_out,
        gain_attn.reshape(1, feat),
        router_t,
        expert_ids.T,
        lengths,
        placement,
        w_gate_up.transpose(0, 1, 3, 2),
        w_down,
    )
    return (
        combined.astype(BF16),
        (combined * scale * gain_final).astype(BF16),
    )


def solution(mesh):
    placed = (
        P("req", "tp"),
        P("req", "tp"),
        P("tp", None),
        P("tp"),
        P("tp", None),
        P("req", None),
        P("req", None),
        P(),
        P("req", None, None, "tp"),
        P("req", "tp", None),
        P("tp"),
    )
    return jax.shard_map(
        on_device,
        mesh=mesh,
        in_specs=placed,
        out_specs=(P("req", "tp"), P("req", "tp")),
        check_vma=False,
    )
```
